32 devices in a mesh: grp: 1, dev: 32 (over z, y, x, core).
Axes of the slice: x: 2, y: 2, z: 4, core: 2. Of those that a mesh axis runs over, the one named last changes fastest.
Arguments:
- hidden_in: bfloat16 [640, 32, 768], P(('grp', 'dev')), may hold values from -6 to 6
- grad_out: bfloat16 [640, 32, 768], P(('grp', 'dev')), may hold values from -6 to 6
- norm_gain: float32 [768], replicated, may hold values from 0.25 to 1.75
- w_qkv: bfloat16 [768, 2304], replicated, may hold values from -0.21875 to 0.21875
- w_out: bfloat16 [768, 768], replicated, may hold values from -0.21875 to 0.21875
- sharpness: float32 [12], replicated, may hold values from 4 to 20
- cohort_ids: int32 [640], P('grp'), may hold values from 0 to 3
- observed: int32 [640, 32], P('grp', 'dev'), may hold values 0 or 1
Outputs:
- grad_in: bfloat16 [640, 32, 768], P(('grp', 'dev'))
- grad_qkv: float32 [768, 2304], P(('grp', 'dev'))
- grad_wout: float32 [768, 768], P(('grp', 'dev'))
The draws below stay inside these ranges and needn't reach their ends.
All inputs are finite; a program needn't handle non-finite values. No bound on the sum of `observed` on one device may be relied on, other than what follows from the above.
Results may differ from the reference program's by a relative error of at most 0.015.
Values may be sent and summed in bfloat16 or wider, within the bound.
A program may use at most 128 MiB of HBM per device.

```python
import math
import jax
import jax.numpy as jnp
from jax import lax

D = 768
H = 12
COHORTS = 4
C = 640
P_SIZE = 32
N_DEV = 32


def touch_ends(values, key, least, largest):
    spot = [jax.random.randint(jax.random.fold_in(key, axis), (), 0, length) for axis, length in enumerate(values.shape)]
    longest = values.shape.index(max(values.shape))
    next_to = spot[:longest] + [(spot[longest] + 1) % values.shape[longest]] + spot[longest + 1:]
    return values.at[tuple(spot)].set(least).at[tuple(next_to)].set(largest)


def steps_of(stream_key, extent, split, least, largest):
    loudness, own = 1.0, jax.random.fold_in(stream_key, 6)
    for axis_at, parts in split:
        draws = jnp.exp(jax.random.uniform(jax.random.fold_in(own, axis_at), (parts,), jnp.float32, least / len(split), largest / len(split)))
        loudness = loudness * jnp.repeat(draws, extent[axis_at] // parts).reshape([-1 if axis == axis_at else 1 for axis in range(len(extent))])
    return loudness


def noise(stream_key, shape, deviation, bound, cuts=(), kind=jnp.bfloat16):
    factor_of = steps_of(stream_key, shape, cuts, -0.22, 0.18) if cuts else 1.0
    array = jax.random.normal(stream_key, shape, jnp.float32) * deviation * factor_of
    return jnp.minimum(jnp.maximum(array, -bound), bound).astype(kind)


def setup_inputs(seed: int = 0, part: int = 0) -> dict:
    key_list = jax.random.split(jax.random.key(seed), 9)
    own_keys = jax.random.split(jax.random.fold_in(key_list[8], part), 9)
    hidden_in = noise(own_keys[0], (C, P_SIZE, D), 1.0, 6.0, ((0, 32),))
    grad_out = noise(own_keys[1], (C, P_SIZE, D), 1.0, 6.0, ((0, 32),))
    norm_gain = jnp.clip(1.0 + 0.15 * jax.random.normal(key_list[2], (D,), jnp.float32), 0.25, 1.75)
    w_qkv = noise(key_list[3], (D, 3 * D), D ** -0.5, 0.21875)
    w_out = noise(key_list[4], (D, D), D ** -0.5, 0.21875)
    sharpness = jnp.clip(jnp.exp(jax.random.uniform(key_list[5], (H,), jnp.float32, math.log(4.0), math.log(20.0))), 4.0, 20.0)
    cohort_ids = touch_ends(jax.random.randint(own_keys[6], (C,), 0, COHORTS), jax.random.fold_in(own_keys[6], 1), 0, COHORTS - 1).astype(jnp.int32)
    observed = touch_ends((jax.random.randint(own_keys[7], (C, P_SIZE), 0, 4) < 3).astype(jnp.int32), jax.random.fold_in(own_keys[7], 1), 0, 1)
    return dict(hidden_in=hidden_in, grad_out=grad_out, norm_gain=norm_gain, w_qkv=w_qkv, w_out=w_out, sharpness=sharpness, cohort_ids=cohort_ids, observed=observed)


epsilon = 1e-06

def block_grads(rows_in, grad_rows, observed_block, norm_gain, w_qkv, w_out, sharpness, cohort_ids):
    campaigns, patches, width = rows_in.shape
    heads = sharpness.shape[0]
    head_size = width // heads
    values = rows_in.astype(jnp.float32)
    inv_rms = lax.rsqrt(lax.optimization_barrier(jnp.mean(values * values, axis=-1, keepdims=True)) + epsilon)
    unit_rows = values * inv_rms
    normed = (unit_rows * norm_gain).astype(jnp.bfloat16).reshape(-1, width)
    projected = jnp.dot(normed, w_qkv, preferred_element_type=jnp.float32)
    shape4 = (campaigns, patches, heads, head_size)
    query_raw = projected[:, :width].reshape(shape4)
    key_raw = projected[:, width:2 * width].reshape(shape4)
    value_raw = projected[:, 2 * width:].reshape(shape4)
    query_inv = lax.rsqrt(lax.optimization_barrier(jnp.mean(query_raw * query_raw, axis=-1, keepdims=True)) + epsilon)
    key_inv = lax.rsqrt(lax.optimization_barrier(jnp.mean(key_raw * key_raw, axis=-1, keepdims=True)) + epsilon)
    query_unit = query_raw * query_inv
    key_unit = key_raw * key_inv
    query_half = query_unit.astype(jnp.bfloat16).astype(jnp.float32)
    key_half = key_unit.astype(jnp.bfloat16).astype(jnp.float32)
    value_half = value_raw.astype(jnp.bfloat16).astype(jnp.float32)
    dy_rows = grad_rows.reshape(-1, width)
    grad_attn = lax.dot_general(dy_rows, w_out, (((1,), (1,)), ((), ())), preferred_element_type=jnp.float32)
    grad_attn = grad_attn.astype(jnp.bfloat16).astype(jnp.float32).reshape(shape4)
    same = cohort_ids[:, None] == cohort_ids[None, :]
    diagonal = jnp.eye(campaigns, dtype=bool)
    keys_seen = (observed_block.T == 1)[:, None, :]
    allowed = jnp.where(same[None] & (keys_seen | diagonal[None]), 1.0, 0.0).astype(jnp.float32)
    scale = (sharpness / head_size)[:, None, None, None]
    scores = jnp.einsum('iphe,jphe->hpij', query_half, key_half) * scale
    raw_weights = jnp.exp(scores) * allowed[None]
    probs = raw_weights / lax.optimization_barrier(jnp.sum(raw_weights, axis=-1, keepdims=True))
    probs_half = probs.astype(jnp.bfloat16).astype(jnp.float32)
    attended = jnp.einsum('hpij,jphe->iphe', probs_half, value_half)
    grad_probs = jnp.einsum('iphe,jphe->hpij', grad_attn, value_half)
    grad_value = jnp.einsum('hpij,iphe->jphe', probs_half, grad_attn)
    row_dot = lax.optimization_barrier(jnp.sum(grad_probs * probs, axis=-1, keepdims=True))
    grad_scores = (probs * (grad_probs - row_dot) * scale).astype(jnp.bfloat16).astype(jnp.float32)
    grad_qunit = jnp.einsum('hpij,jphe->iphe', grad_scores, key_half)
    grad_kunit = jnp.einsum('hpij,iphe->jphe', grad_scores, query_half)
    grad_query = query_inv * (grad_qunit - query_unit * lax.optimization_barrier(jnp.mean(grad_qunit * query_unit, axis=-1, keepdims=True)))
    grad_key = key_inv * (grad_kunit - key_unit * lax.optimization_barrier(jnp.mean(grad_kunit * key_unit, axis=-1, keepdims=True)))
    grad_proj = jnp.concatenate([grad_query.reshape(-1, width), grad_key.reshape(-1, width), grad_value.reshape(-1, width)], axis=1).astype(jnp.bfloat16)
    attended_half = attended.astype(jnp.bfloat16).reshape(-1, width)
    out_term = lax.dot_general(attended_half, dy_rows, (((0,), (0,)), ((), ())), preferred_element_type=jnp.float32)
    qkv_term = lax.dot_general(normed, grad_proj, (((0,), (0,)), ((), ())), preferred_element_type=jnp.float32)
    grad_normed = lax.dot_general(grad_proj, w_qkv, (((1,), (1,)), ((), ())), preferred_element_type=jnp.float32)
    shaped = grad_normed.reshape(campaigns, patches, width) * norm_gain
    result = grad_rows.astype(jnp.float32) + inv_rms * (shaped - unit_rows * lax.optimization_barrier(jnp.mean(shaped * unit_rows, axis=-1, keepdims=True)))
    return (result.astype(jnp.bfloat16), qkv_term, out_term)

def reference(hidden_in, grad_out, norm_gain, w_qkv, w_out, sharpness, cohort_ids, observed):
    campaigns, patches, width = hidden_in.shape
    per_block = patches // N_DEV

    def step(carry, block):
        start = (block * per_block).astype(jnp.int32)
        rows_in = lax.dynamic_slice_in_dim(hidden_in, start, per_block, 1)
        grad_rows = lax.dynamic_slice_in_dim(grad_out, start, per_block, 1)
        observed_block = lax.dynamic_slice_in_dim(observed, start, per_block, 1)
        result, qkv_term, out_term = block_grads(rows_in, grad_rows, observed_block, norm_gain, w_qkv, w_out, sharpness, cohort_ids)
        qkv_round = lax.optimization_barrier(qkv_term.astype(jnp.bfloat16)).astype(jnp.float32)
        out_round = lax.optimization_barrier(out_term.astype(jnp.bfloat16)).astype(jnp.float32)
        return ((carry[0] + qkv_round, carry[1] + out_round), result)
    start_sums = (jnp.zeros((width, 3 * width), jnp.float32), jnp.zeros((width, width), jnp.float32))
    sums, results = lax.scan(step, start_sums, jnp.arange(N_DEV, dtype=jnp.int32))
    grad_in = jnp.moveaxis(results, 0, 1).reshape(campaigns, patches, width)
    return (grad_in, sums[0], sums[1])
```

```python
import functools
import math

import jax
import jax.numpy as jnp
from jax import lax
from jax.experimental import pallas as pl
from jax.experimental.pallas import tpu as pltpu
from jax.sharding import PartitionSpec as P

epsilon = 1e-06
log2e = math.log2(math.e)
cohort_kinds = 4


def dot(left, right, dims):
    return lax.dot_general(left, right, ((dims[0], dims[1]), ((), ())), preferred_element_type=jnp.float32)


def forward_kernel(
    head_size,
    group,
    sharp_ref,
    x_ref,
    gain_ref,
    wq_ref,
    wk_ref,
    wv_ref,
    cohort_col_ref,
    cohort_row_ref,
    seen_ref,
    normed_t_ref,
    q_ref,
    k_ref,
    k_t_ref,
    v_ref,
    inv_ref,
    probs_ref,
    att_ref,
    normed_ref,
    mask_ref,
):
    step = pl.program_id(0)
    rows, width = x_ref.shape

    @pl.when(step == 0)
    def _():
        values = x_ref[...].astype(jnp.float32)
        inv = lax.rsqrt(jnp.mean(values * values, axis=-1, keepdims=True) + epsilon)
        normed = values * inv * gain_ref[...]
        normed_ref[...] = normed.astype(jnp.bfloat16)
        normed_t_ref[...] = normed.T.astype(jnp.bfloat16)
        same = cohort_col_ref[...] == cohort_row_ref[...]
        diagonal = lax.broadcasted_iota(jnp.int32, (rows, rows), 0) == lax.broadcasted_iota(
            jnp.int32, (rows, rows), 1
        )
        seen = jnp.broadcast_to(seen_ref[...], (rows, rows)) == 1
        mask_ref[...] = jnp.where(same & (seen | diagonal), 1.0, 0.0)

    normed = normed_ref[...]
    q_raw = dot(normed, wq_ref[...], ((1,), (0,)))
    k_raw = dot(normed, wk_ref[...], ((1,), (0,)))
    v_raw = dot(normed, wv_ref[...], ((1,), (0,)))
    v_ref[...] = v_raw.astype(jnp.bfloat16)
    for h in range(group):
        base = h * head_size
        lanes = slice(base, base + head_size)
        q = q_raw[:, lanes]
        k = k_raw[:, lanes]
        v_t = v_raw[:, lanes].T.astype(jnp.bfloat16)
        q_inv = lax.rsqrt(jnp.mean(q * q, axis=-1, keepdims=True) + epsilon)
        k_inv = lax.rsqrt(jnp.mean(k * k, axis=-1, keepdims=True) + epsilon)
        q_half = (q * q_inv).astype(jnp.bfloat16)
        k_unit = k * k_inv
        k_half = k_unit.astype(jnp.bfloat16)
        k_t_ref[lanes, :] = k_unit.T.astype(jnp.bfloat16)
        q_ref[:, lanes] = q_half
        k_ref[:, lanes] = k_half
        inv_ref[0, :, h : h + 1] = q_inv
        inv_ref[0, :, group + h : group + h + 1] = k_inv
        scale = sharp_ref[step * group + h] / head_size
        scores = dot(k_half, q_half, ((1,), (1,)))
        weights = jnp.exp2(scores * (scale * log2e)) * mask_ref[...]
        probs = weights * (1.0 / jnp.sum(weights, axis=0, keepdims=True))
        probs_half = probs.astype(jnp.bfloat16)
        probs_ref[h] = probs_half
        att_ref[base : base + head_size, :] = dot(v_t, probs_half, ((1,), (0,))).astype(jnp.bfloat16)


def backward_kernel(
    head_size,
    group,
    sharp_ref,
    x_ref,
    dy_ref,
    gain_ref,
    wqkv_t_ref,
    wo_t_ref,
    q_ref,
    k_ref,
    k_t_ref,
    v_ref,
    inv_ref,
    probs_ref,
    gin_ref,
    dproj_ref,
):
    step = pl.program_id(0)
    gw = group * head_size
    width = x_ref.shape[1]
    da_half = dot(dy_ref[...], wo_t_ref[...], ((1,), (0,))).astype(jnp.bfloat16)
    parts = ([], [], [])
    for h in range(group):
        base = h * head_size
        lanes = slice(base, base + head_size)
        q_half = q_ref[:, lanes]
        q_unit = q_half.astype(jnp.float32)
        k_unit = k_ref[:, lanes].astype(jnp.float32)
        da = da_half[:, lanes]
        q_inv = inv_ref[0, :, h : h + 1]
        k_inv = inv_ref[0, :, group + h : group + h + 1]
        scale = sharp_ref[step * group + h] / head_size
        grad_probs = dot(v_ref[:, lanes], da, ((1,), (1,)))
        probs_half = probs_ref[h]
        probs = probs_half.astype(jnp.float32)
        grad_v = dot(probs_half, da, ((1,), (0,)))
        row_dot = jnp.sum(grad_probs * probs, axis=0, keepdims=True)
        grad_scores = (probs * (grad_probs - row_dot)).astype(jnp.bfloat16)
        dq = dot(k_t_ref[lanes, :], grad_scores, ((1,), (0,))).T * scale
        dk = dot(grad_scores, q_half, ((1,), (0,))) * scale
        dq = q_inv * (dq - q_unit * jnp.mean(dq * q_unit, axis=-1, keepdims=True))
        dk = k_inv * (dk - k_unit * jnp.mean(dk * k_unit, axis=-1, keepdims=True))
        for part, value in zip(parts, (dq, dk, grad_v)):
            part.append(value.astype(jnp.bfloat16))
    for at, part in enumerate(parts):
        start = pl.multiple_of(at * width + step * gw, gw)
        dproj_ref[:, pl.ds(start, gw)] = jnp.concatenate(part, axis=1)

    @pl.when(step == pl.num_programs(0) - 1)
    def _():
        values = x_ref[...].astype(jnp.float32)
        inv = lax.rsqrt(jnp.mean(values * values, axis=-1, keepdims=True) + epsilon)
        unit = values * inv
        shaped = dot(dproj_ref[...], wqkv_t_ref[...], ((1,), (0,))) * gain_ref[...]
        result = dy_ref[...].astype(jnp.float32) + inv * (
            shaped - unit * jnp.mean(shaped * unit, axis=-1, keepdims=True)
        )
        gin_ref[...] = result.astype(jnp.bfloat16)


def weights_kernel(normed_t_ref, att_ref, dq_ref, dk_ref, dv_ref, dy_ref, gqkv_ref, gwo_ref):
    dproj = jnp.concatenate([dq_ref[...], dk_ref[...], dv_ref[...]], axis=1)
    gqkv_ref[0] = dot(normed_t_ref[...], dproj, ((1,), (0,))).astype(jnp.bfloat16)
    gwo_ref[...] = dot(att_ref[...], dy_ref[...], ((1,), (0,))).astype(jnp.bfloat16)


def patch_grads(x, dy, norm_gain, w_qkv, w_out, sharpness, cohort_ids, seen):
    rows, width = x.shape
    heads = sharpness.shape[0]
    head_size = width // heads
    group = math.gcd(heads, 2)
    steps = heads // group
    gw = group * head_size
    half = jnp.bfloat16
    whole = lambda shape: pl.BlockSpec(shape, lambda g: (0,) * len(shape))
    cols = lambda n: pl.BlockSpec((rows, n), lambda g: (0, g))
    lines = lambda n: pl.BlockSpec((gw, n), lambda g: (g, 0))
    smem = pl.BlockSpec(memory_space=pltpu.SMEM)
    weights = [
        pl.BlockSpec((width, gw), lambda g: (0, g)),
        pl.BlockSpec((width, gw), lambda g: (0, steps + g)),
        pl.BlockSpec((width, gw), lambda g: (0, 2 * steps + g)),
    ]
    invs = pl.BlockSpec((1, rows, 2 * group), lambda g: (g, 0, 0))
    probs_spec = pl.BlockSpec((group, rows, rows), lambda g: (g, 0, 0))
    w_qkv_t, w_out_t = w_qkv.T, w_out.T
    params = pltpu.CompilerParams(vmem_limit_bytes=60 * 1024 * 1024)

    def cost(flops):
        return pl.CostEstimate(flops=flops, bytes_accessed=rows * width * 20, transcendentals=0)

    forward = pl.pallas_call(
        functools.partial(forward_kernel, head_size, group),
        grid=(steps,),
        in_specs=[smem, whole((rows, width)), whole((1, width))]
        + weights
        + [whole((rows, 1)), whole((1, rows)), whole((rows, 1))],
        out_specs=[whole((width, rows)), cols(gw), cols(gw), lines(rows), cols(gw), invs, probs_spec, lines(rows)],
        out_shape=[
            jax.ShapeDtypeStruct((width, rows), half),
            jax.ShapeDtypeStruct((rows, width), half),
            jax.ShapeDtypeStruct((rows, width), half),
            jax.ShapeDtypeStruct((width, rows), half),
            jax.ShapeDtypeStruct((rows, width), half),
            jax.ShapeDtypeStruct((steps, rows, 2 * group), jnp.float32),
            jax.ShapeDtypeStruct((heads, rows, rows), half),
            jax.ShapeDtypeStruct((width, rows), half),
        ],
        scratch_shapes=[
            pltpu.VMEM((rows, width), half),
            pltpu.VMEM((rows, rows), jnp.float32),
        ],
        compiler_params=params,
        cost_estimate=cost(40_000_000_000),
    )
    with jax.named_scope("forward_part"):
        normed_t, q, k, k_t, v, inv, probs, att = forward(
            sharpness,
            x,
            norm_gain[None, :],
            w_qkv,
            w_qkv,
            w_qkv,
            cohort_ids[:, None],
            cohort_ids[None, :],
            seen,
        )
    gin, dproj = pl.pallas_call(
        functools.partial(backward_kernel, head_size, group),
        grid=(steps,),
        in_specs=[
            smem,
            whole((rows, width)),
            whole((rows, width)),
            whole((1, width)),
            whole((3 * width, width)),
            pl.BlockSpec((width, gw), lambda g: (0, g)),
            cols(gw),
            cols(gw),
            lines(rows),
            cols(gw),
            invs,
            probs_spec,
        ],
        out_specs=[whole((rows, width)), whole((rows, 3 * width))],
        out_shape=[
            jax.ShapeDtypeStruct((rows, width), half),
            jax.ShapeDtypeStruct((rows, 3 * width), half),
        ],
        compiler_params=params,
        cost_estimate=cost(25_000_000_000),
    )(sharpness, x, dy, norm_gain[None, :], w_qkv_t, w_out_t, q, k, k_t, v, inv, probs)
    gqkv, gwo = pl.pallas_call(
        weights_kernel,
        grid=(steps,),
        in_specs=[
            whole((width, rows)),
            lines(rows),
            cols(gw),
            pl.BlockSpec((rows, gw), lambda g: (0, steps + g)),
            pl.BlockSpec((rows, gw), lambda g: (0, 2 * steps + g)),
            whole((rows, width)),
        ],
        out_specs=[pl.BlockSpec((1, width, 3 * gw), lambda g: (g, 0, 0)), lines(width)],
        out_shape=[
            jax.ShapeDtypeStruct((steps, width, 3 * gw), half),
            jax.ShapeDtypeStruct((width, width), half),
        ],
        compiler_params=pltpu.CompilerParams(vmem_limit_bytes=30 * 1024 * 1024),
        cost_estimate=cost(8_000_000_000),
    )(normed_t, att, dproj, dproj, dproj, dy)
    return gin, gqkv, gwo


def scatter_kernel(n, chunks, group_cols, qkv_ref, wo_ref, out_ref, wout_ref, *scratch):
    bits = n.bit_length() - 1
    recv = scratch[:bits]
    kept = (None,) + scratch[bits : 2 * bits - 1]
    send_sem, recv_sem = scratch[2 * bits - 1 :]
    me = lax.axis_index("dev")
    bit = [(me // (1 << b)) % 2 for b in range(bits)]
    peer = [me + (1 - 2 * bit[b]) * (1 << b) for b in range(bits)]
    groups = qkv_ref.shape[0]
    cols = qkv_ref.shape[-1]
    width = wout_ref.shape[-1]

    barrier = pltpu.get_barrier_semaphore()
    for b in range(bits):
        pl.semaphore_signal(
            barrier, inc=1, device_id={"dev": peer[b]}, device_id_type=pl.DeviceIdType.MESH
        )
    pl.semaphore_wait(barrier, bits)

    def order_of(chunk):
        order = list(range(bits))
        if chunk % 2 and bits > 2:
            order[1], order[2] = order[2], order[1]
        return order

    def source(chunk, phase, side):
        order = order_of(chunk)
        left = sorted(set(range(bits)) - set(order[:phase]), reverse=True)
        picks = tuple(side if b == order[phase] else slice(None) for b in left)
        if phase:
            return kept[phase], (chunk,) + picks
        if chunk < groups:
            return qkv_ref, (chunk,) + picks
        start = (chunk - groups) * cols
        return wo_ref, picks + (slice(None), slice(start, start + cols))

    copies = {}

    def begin(chunk, phase):
        b = order_of(chunk)[phase]
        ref, index = source(chunk, phase, 1 - bit[b])
        copy = pltpu.make_async_remote_copy(
            src_ref=ref.at[index],
            dst_ref=recv[phase].at[chunk],
            send_sem=send_sem.at[chunk, phase],
            recv_sem=recv_sem.at[chunk, phase],
            device_id={"dev": peer[b]},
            device_id_type=pl.DeviceIdType.MESH,
        )
        copy.start()
        copies[chunk, phase] = copy

    def finish(chunk, phase):
        b = order_of(chunk)[phase]
        copies[chunk, phase].wait_recv()
        ref, index = source(chunk, phase, bit[b])
        total = ref[index].astype(jnp.float32) + recv[phase][chunk].astype(jnp.float32)
        if phase + 1 < bits:
            kept[phase + 1][chunk] = total.astype(jnp.bfloat16)
            begin(chunk, phase + 1)
        elif chunk < groups:
            for part in range(3):
                at = part * width + chunk * group_cols
                out_ref[:, at : at + group_cols] = total[
                    :, part * group_cols : (part + 1) * group_cols
                ]
        else:
            at = (chunk - groups) * cols
            wout_ref[:, at : at + cols] = total

    for chunk in range(chunks):
        begin(chunk, 0)
    pairs = -(-chunks // 2)
    for wave in range(pairs + bits - 1):
        for phase in reversed(range(bits)):
            pair = wave - phase
            if 0 <= pair < pairs:
                for chunk in range(2 * pair, min(2 * pair + 2, chunks)):
                    finish(chunk, phase)
    for copy in copies.values():
        copy.wait_send()


def scatter_sums(gqkv, gwo, n):
    groups, width, cols = gqkv.shape
    bits = n.bit_length() - 1
    rows = width // n
    chunks = groups + width // cols
    cube = (2,) * bits
    recv = [pltpu.VMEM((chunks,) + (2,) * (bits - 1 - p) + (rows, cols), jnp.bfloat16) for p in range(bits)]
    kept = [pltpu.VMEM((chunks,) + (2,) * (bits - p) + (rows, cols), jnp.bfloat16) for p in range(1, bits)]
    vmem = pl.BlockSpec(memory_space=pltpu.VMEM)
    return pl.pallas_call(
        functools.partial(scatter_kernel, n, chunks, cols // 3),
        in_specs=[vmem, vmem],
        out_specs=[vmem, vmem],
        out_shape=[
            jax.ShapeDtypeStruct((rows, 3 * width), jnp.float32),
            jax.ShapeDtypeStruct((rows, width), jnp.float32),
        ],
        scratch_shapes=recv
        + kept
        + [pltpu.SemaphoreType.DMA((chunks, bits)), pltpu.SemaphoreType.DMA((chunks, bits))],
        compiler_params=pltpu.CompilerParams(
            collective_id=0, has_side_effects=True, vmem_limit_bytes=40 * 1024 * 1024
        ),
        cost_estimate=pl.CostEstimate(
            flops=40_000_000_000, bytes_accessed=8 * gqkv.size, transcendentals=0
        ),
    )(gqkv.reshape((groups,) + cube + (rows, cols)), gwo.reshape(cube + (rows, width)))


def layer(n, hidden_in, grad_out, norm_gain, w_qkv, w_out, sharpness, cohort_ids, observed):
    width = hidden_in.shape[-1]
    x = lax.all_to_all(hidden_in, "dev", split_axis=1, concat_axis=0, tiled=True)
    with jax.named_scope("cotangent_move"):
        dy = lax.all_to_all(grad_out, "dev", split_axis=1, concat_axis=0, tiled=True)
    campaigns, patches, _ = x.shape
    gin, gqkv, gwo = [], 0.0, 0.0
    for p in range(patches):
        a, b, c = patch_grads(
            x[:, p], dy[:, p], norm_gain, w_qkv, w_out, sharpness, cohort_ids, observed[:, p : p + 1]
        )
        gin.append(a.reshape(n, campaigns // n, width))
        gqkv, gwo = (b, c) if p == 0 else (gqkv + b, gwo + c)
    gin = gin[0] if patches == 1 else jnp.stack(gin, axis=1).reshape(n * patches, campaigns // n, width)
    grad_in = lax.all_to_all(gin, "dev", split_axis=0, concat_axis=0, tiled=True).transpose(1, 0, 2)
    grad_qkv, grad_wout = scatter_sums(gqkv, gwo, n)
    return (grad_in, grad_qkv, grad_wout)


def steps_to(total, body):
    lax.fori_loop(0, total, lambda i, c: (body(i), c)[1], 0)


def fused_kernel(
    n,
    block,
    cohorts,
    head_size,
    sharp_ref,
    x_hbm,
    dy_hbm,
    wqkv_hbm,
    wo_hbm,
    gain_ref,
    cohort_ref,
    seen_ref,
    gin_ref,
    gqkv_ref,
    gwo_ref,
    x_in,
    dy_in,
    wqkv_ref,
    wo_ref,
    flat,
    x_out,
    dy_out,
    x_got,
    dy_got,
    gin_got,
    tail_ref,
    got_ref,
    place_ref,
    place_t_ref,
    mask_ref,
    xs_ref,
    normed_ref,
    normed_t_ref,
    q_ref,
    k_ref,
    v_ref,
    q_inv_ref,
    k_inv_ref,
    probs_ref,
    att_ref,
    dys_ref,
    da_ref,
    dproj_ref,
    sums_ref,
    *rest,
):
    bits = n.bit_length() - 1
    recv = rest[:bits]
    local_sem, send_sem, recv_sem, sum_send, sum_recv = rest[bits:]
    half, full = jnp.bfloat16, jnp.float32
    per, patches, width = x_in.shape
    campaigns = per * n
    lanes = 128
    cuts = width // lanes
    middle = width // 2
    rows = block * cohorts
    heads = width // head_size
    pair = lanes // head_size
    groups = heads // pair
    wide = pair * block
    major = per - per % 16
    minor = per % 16
    tiles = major // 8
    spread = per + 8 - per % 8
    log_heads = groups
    me = lax.axis_index("dev")

    def other(i):
        return lax.rem(me + i, n)

    def before(i):
        return lax.rem(me + n - i, n)

    loads = [
        pltpu.make_async_copy(a, b, local_sem.at[i])
        for i, (a, b) in enumerate(((x_hbm, x_in), (dy_hbm, dy_in), (wqkv_hbm, wqkv_ref), (wo_hbm, wo_ref)))
    ]
    for load in loads:
        load.start()
    barrier = pltpu.get_barrier_semaphore()

    def greet(i):
        pl.semaphore_signal(
            barrier, inc=1, device_id={"dev": other(i + 1)}, device_id_type=pl.DeviceIdType.MESH
        )

    steps_to(n - 1, greet)

    def prepare(source, out):
        def widen(c):
            start = pl.multiple_of(c * patches, 8)
            for b in range(cuts):
                flat[b, pl.ds(start, patches), :] = source[c, :, b * lanes : (b + 1) * lanes].astype(full)

        def pick(p):
            for b in range(cuts):
                to, at = divmod(b, cuts // 2)
                at = slice(at * lanes, (at + 1) * lanes)
                body = flat[b, pl.ds(p, major, stride=patches), :].reshape(tiles, 8, lanes)
                out[p, to * tiles : (to + 1) * tiles, :, at] = body.astype(half)
            ends = []
            for b in range(cuts):
                ends.append(flat[b, pl.ds(major * patches + p, minor, stride=patches), :])
            for b in range(cuts // 2):
                both = jnp.concatenate([ends[b], ends[b + cuts // 2]], axis=0)
                out[p, 2 * tiles, :, b * lanes : (b + 1) * lanes] = both.astype(half)

        steps_to(per, widen)
        steps_to(n, pick)

    def transfer(kind, out, got, to, slot):
        return pltpu.make_async_remote_copy(
            src_ref=out.at[to],
            dst_ref=got.at[slot],
            send_sem=send_sem.at[kind, to],
            recv_sem=recv_sem.at[kind, slot],
            device_id={"dev": to},
            device_id_type=pl.DeviceIdType.MESH,
        )

    def send_all(kind, out, got):
        steps_to(n - 1, lambda i: transfer(kind, out, got, other(i + 1), me).start())

    def sent_all(kind, out, got):
        steps_to(n - 1, lambda i: transfer(kind, out, got, other(i + 1), me).wait_send())

    def arrived(kind, out, got, source):
        transfer(kind, out, got, source, source).wait_recv()

    loads[0].wait()
    prepare(x_in, x_out)
    pl.semaphore_wait(barrier, n - 1)
    send_all(0, x_out, x_got)
    x_got[me] = x_out[me]
    loads[1].wait()
    prepare(dy_in, dy_out)
    dy_got[me] = dy_out[me]
    send_all(1, dy_out, dy_got)

    cohort = cohort_ref[...]
    line8 = jnp.broadcast_to(cohort.astype(full), (8, campaigns))
    column = line8.T[:, 0:1]
    same = (column == cohort.astype(full)) & (
        lax.broadcasted_iota(jnp.int32, (campaigns, campaigns), 0)
        < lax.broadcasted_iota(jnp.int32, (campaigns, campaigns), 1)
    )
    rank = jnp.sum(jnp.where(same, 1.0, 0.0), axis=0, keepdims=True)
    spot = cohort.astype(full) * block + rank
    high = jnp.floor(spot * (1 / 16))
    low = spot - 16 * high
    tags = jnp.concatenate(
        [high, low, seen_ref[...].astype(full), jnp.zeros((5, campaigns), full)], axis=0
    ).astype(half)
    slots = n * (major + 8)
    slot = lax.broadcasted_iota(jnp.int32, (1, slots), 1)
    after = slot - n * major
    in_major = slot < n * major
    first = in_major | (after % 8 < 4)
    owner = jnp.where(
        in_major, (slot // major) * per + slot % major, (after // 8) * per + major + after % minor
    )
    pick = jnp.where(lax.broadcasted_iota(jnp.int32, (campaigns, slots), 0) == owner, 1.0, 0.0)
    tags = dot(tags, pick.astype(half), ((1,), (0,)))
    spot = 16 * tags[0:1] + tags[1:2]
    spot8 = jnp.broadcast_to(spot, (8, slots))
    place = jnp.where(lax.broadcasted_iota(jnp.int32, (rows, slots), 0).astype(full) == spot, 1.0, 0.0)
    place_ref[...] = place.astype(half)
    place_t = jnp.where(lax.broadcasted_iota(jnp.int32, (slots, rows), 1).astype(full) == spot8.T[:, 0:1], 1.0, 0.0)
    place_t_ref[...] = place_t.astype(half)
    known = jnp.where(first, tags[2:3], 0.0)
    known = dot(place_ref[...], jnp.broadcast_to(known, (8, slots)).astype(half), ((1,), (1,)))[:, 0:1]
    for c in range(cohorts):
        row = lax.broadcasted_iota(jnp.int32, (block, block), 0)
        col = lax.broadcasted_iota(jnp.int32, (block, block), 1)
        mine = jnp.broadcast_to(known[c * block : (c + 1) * block], (block, block))
        square = jnp.where((row == col) | (mine > 0.5), 1.0, 0.0)
        mask_ref[c * block : (c + 1) * block, :] = jnp.concatenate([square] * pair, axis=1)

    lane = lax.broadcasted_iota(jnp.int32, (1, lanes), 1)
    ones_row = lax.broadcasted_iota(jnp.int32, (2 * lanes, lanes), 0) % lanes // head_size
    ones_col = lax.broadcasted_iota(jnp.int32, (2 * lanes, lanes), 1) // head_size
    ones = jnp.where(ones_row == ones_col, 1.0 / head_size, 0.0).astype(half)

    def head_mean(values):
        upper = values.astype(half)
        lower = (values - upper.astype(full)).astype(half)
        return dot(jnp.concatenate([upper, lower], axis=1), ones, ((1,), (0,)))

    def split(values):
        return jnp.concatenate(
            [jnp.where(lane // head_size == h, values, jnp.zeros_like(values)) for h in range(pair)], axis=0
        )

    def gather(kind, out, got):
        def take(source):
            values = got[source].astype(full)
            start = pl.multiple_of(source * major, 16)
            got_ref[pl.ds(start, major), 0:middle] = values[0:tiles].reshape(major, middle).astype(half)
            got_ref[pl.ds(start, major), middle:width] = (
                values[tiles : 2 * tiles].reshape(major, middle).astype(half)
            )
            tail_ref[pl.ds(pl.multiple_of(source * 8, 8), 8), :] = values[2 * tiles]

        def step(i):
            source = before(i + 1)
            arrived(kind, out, got, source)
            take(source)

        take(me)
        steps_to(n - 1, step)
        ends = tail_ref[...]
        upper = lax.broadcasted_iota(jnp.int32, ends.shape, 0) % 8 < 4
        start = n * major
        got_ref[start:, 0:middle] = jnp.where(upper, ends, 0.0).astype(half)
        got_ref[start:, middle:width] = jnp.where(upper, 0.0, ends).astype(half)

    loads[2].wait()
    loads[3].wait()
    gather(0, x_out, x_got)

    def settle(c):
        at = pl.ds(pl.multiple_of(c * block, block), block)
        values = dot(place_ref[at, :], got_ref[...], ((1,), (0,)))
        xs_ref[at, :] = values.astype(half)
        inv = lax.rsqrt(jnp.mean(values * values, axis=-1, keepdims=True) + epsilon)
        normed_ref[at, :] = (values * inv * gain_ref[...]).astype(half)

    steps_to(cohorts, settle)

    def turn(b):
        at = pl.ds(pl.multiple_of(b * lanes, lanes), lanes)
        normed_t_ref[at, :] = normed_ref[:, at].astype(full).T.astype(half)

    def project(g):
        def raw(part):
            at = pl.ds(pl.multiple_of(part * width + g * lanes, lanes), lanes)
            return dot(normed_ref[...], wqkv_ref[:, at], ((1,), (0,)))

        at = pl.ds(pl.multiple_of(g * lanes, lanes), lanes)
        for part, (unit_ref, inv_ref) in enumerate(((q_ref, q_inv_ref), (k_ref, k_inv_ref))):
            values = raw(part)
            inv = lax.rsqrt(head_mean(values * values) + epsilon)
            unit_ref[:, at] = (values * inv).astype(half)
            inv_ref[:, at] = inv
        v_ref[:, at] = raw(2).astype(half)

    steps_to(groups, project)
    steps_to(cuts, turn)

    def scale_of(g, axis, size):
        shape = (1, size) if axis else (size, 1)
        index = lax.broadcasted_iota(jnp.int32, shape, axis)
        scale = jnp.zeros(shape, full)
        for h in range(pair):
            scale = jnp.where(index // (size // pair) == h, sharp_ref[g * pair + h] / head_size, scale)
        return scale

    def fold(values):
        return jnp.concatenate(
            [
                values[h * head_size : (h + 1) * head_size, h * block : (h + 1) * block]
                for h in range(pair)
            ],
            axis=0,
        )

    def attend(g):
        at = pl.ds(pl.multiple_of(g * lanes, lanes), lanes)
        scale = scale_of(g, 1, wide) * log2e
        for c in range(cohorts):
            block_rows = slice(c * block, (c + 1) * block)
            scores = dot(k_ref[block_rows, at], split(q_ref[block_rows, at]), ((1,), (1,)))
            weights = jnp.exp2(scores * scale) * mask_ref[block_rows, :]
            probs = (weights * (1.0 / jnp.sum(weights, axis=0, keepdims=True))).astype(half)
            probs_ref[g * cohorts + c] = probs
            att = dot(v_ref[block_rows, at].T, probs, ((1,), (0,)))
            att_ref[c, at, :] = fold(att).astype(half)

    steps_to(groups, attend)

    gather(1, dy_out, dy_got)

    def settle_dy(c):
        at = pl.ds(pl.multiple_of(c * block, block), block)
        dys_ref[at, :] = dot(place_ref[at, :], got_ref[...], ((1,), (0,))).astype(half)

    steps_to(cohorts, settle_dy)

    bit = [(me // (1 << b)) % 2 for b in range(bits)]
    peer = [me + (1 - 2 * bit[b]) * (1 << b) for b in range(bits)]
    piece = sums_ref.shape[1 + bits :]
    chunk_cols = piece[-1]

    def order_of(parity):
        order = list(range(bits))
        if parity and bits > 2:
            order[1], order[2] = order[2], order[1]
        return order

    def view(chunk, parity, phase, side):
        order = order_of(parity)
        index = []
        for b in reversed(range(bits)):
            if b in order[:phase]:
                index.append(bit[b])
            elif b == order[phase]:
                index.append(side)
            else:
                index.append(slice(None))
        return (chunk,) + tuple(index)

    def move(chunk, parity, phase):
        b = order_of(parity)[phase]
        return pltpu.make_async_remote_copy(
            src_ref=sums_ref.at[view(chunk, parity, phase, 1 - bit[b])],
            dst_ref=recv[phase].at[chunk],
            send_sem=sum_send.at[chunk, phase],
            recv_sem=sum_recv.at[chunk, phase],
            device_id={"dev": peer[b]},
            device_id_type=pl.DeviceIdType.MESH,
        )

    def finish(chunk, parity, phase):
        b = order_of(parity)[phase]
        move(chunk, parity, phase).wait_recv()
        index = view(chunk, parity, phase, bit[b])
        total = sums_ref[index].astype(full) + recv[phase][chunk].astype(full)
        if phase + 1 < bits:
            sums_ref[index] = total.astype(half)
            move(chunk, parity, phase + 1).start()
        else:
            return total.reshape(width // n, chunk_cols)

    def keep(chunk, values):
        sums_ref[chunk] = values.reshape((2,) * bits + piece).astype(half)

    outer = width // chunk_cols
    for j in range(outer):
        cols = slice(j * chunk_cols, (j + 1) * chunk_cols)
        total = 0.0
        for c in range(cohorts):
            total += dot(att_ref[c], dys_ref[c * block : (c + 1) * block, cols], ((1,), (0,)))
        keep(j, total)
        move(j, j % 2, 0).start()

    def spread_grad(b):
        at = pl.ds(pl.multiple_of(b * 2 * lanes, 2 * lanes), 2 * lanes)
        da_ref[:, at] = dot(dys_ref[...], wo_ref[at, :], ((1,), (1,))).astype(half)

    steps_to(cuts // 2, spread_grad)

    def back(g):
        at = pl.ds(pl.multiple_of(g * lanes, lanes), lanes)
        scale = scale_of(g, 1, lanes)

        def one(c):
            start = pl.multiple_of(c * block, block)
            block_rows = pl.ds(start, block)
            q, k, v = q_ref[block_rows, at], k_ref[block_rows, at], v_ref[block_rows, at]
            q_split = split(q)
            da_split = split(da_ref[block_rows, at])
            grad_probs = dot(v, da_split, ((1,), (1,)))
            probs_half = probs_ref[g * cohorts + c]
            probs = probs_half.astype(full)
            grad_v = dot(probs_half, da_split, ((1,), (0,)))
            row_dot = jnp.sum(grad_probs * probs, axis=0, keepdims=True)
            grad_scores = (probs * (grad_probs - row_dot)).astype(half)
            dk = dot(grad_scores, q_split, ((1,), (0,))) * scale
            dq = fold(dot(k.T, grad_scores, ((1,), (0,)))).T * scale
            for part, (value, unit, inv_ref) in enumerate(((dq, q, q_inv_ref), (dk, k, k_inv_ref))):
                unit = unit.astype(full)
                value = inv_ref[block_rows, at] * (value - unit * head_mean(value * unit))
                to = pl.ds(pl.multiple_of(part * width + g * lanes, lanes), lanes)
                dproj_ref[block_rows, to] = value.astype(half)
            to = pl.ds(pl.multiple_of(2 * width + g * lanes, lanes), lanes)
            dproj_ref[block_rows, to] = grad_v.astype(half)

        for c in range(cohorts):
            one(c)
        parts = [
            dproj_ref[:, pl.ds(pl.multiple_of(part * width + g * lanes, lanes), lanes)] for part in range(3)
        ]
        keep(outer + g, dot(normed_t_ref[...], jnp.concatenate(parts, axis=1), ((1,), (0,))))

    chunks = outer + groups
    turns = groups // 2

    def stage(t):
        for j in range(2):
            g = 2 * t + j
            back(g)
            move(outer + g, j, 0).start()
        for phase in reversed(range(min(bits, turns))):

            @pl.when(t >= phase)
            def _():
                for j in range(2):
                    finish(2 * (t - phase) + j, j, phase)

    steps_to(turns, stage)

    def wave(w):
        for phase in reversed(range(bits)):
            at = w - phase
            if 0 <= at < chunks // 2:
                for j in range(2):
                    chunk = 2 * at + j
                    total = finish(chunk, j, phase)
                    if phase + 1 < bits:
                        continue
                    if chunk < outer:
                        gwo_ref[:, chunk * chunk_cols : (chunk + 1) * chunk_cols] = total
                    else:
                        for part in range(3):
                            start = part * width + (chunk - outer) * lanes
                            gqkv_ref[:, start : start + lanes] = total[:, part * lanes : (part + 1) * lanes]

    def close(c):
        at = pl.ds(pl.multiple_of(c * block, block), block)
        values = xs_ref[at, :].astype(full)
        inv = lax.rsqrt(jnp.mean(values * values, axis=-1, keepdims=True) + epsilon)
        unit = values * inv
        shaped = dot(dproj_ref[at, :], wqkv_ref[...], ((1,), (1,))) * gain_ref[...]
        result = dys_ref[at, :].astype(full) + inv * (
            shaped - unit * jnp.mean(shaped * unit, axis=-1, keepdims=True)
        )
        xs_ref[at, :] = result.astype(half)

    steps_to(cohorts, close)
    sent_all(0, x_out, x_got)
    sent_all(1, dy_out, dy_got)
    quarter = n // 4

    def deliver(i):
        first_to = lax.rem(me // quarter + i, 4) * quarter
        at = pl.ds(pl.multiple_of(first_to * major, quarter * major), quarter * major)
        ends = pl.ds(pl.multiple_of(n * major + first_to * 8, quarter * 8), quarter * 8)
        body = dot(place_t_ref[at, :], xs_ref[...], ((1,), (0,)))
        tail = dot(place_t_ref[ends, :], xs_ref[...], ((1,), (0,)))
        upper = lax.broadcasted_iota(jnp.int32, (quarter * 8, middle), 0) % 8 < 4
        tail = jnp.where(upper, tail[:, 0:middle], tail[:, middle:width])
        x_out[pl.ds(first_to, quarter), 0:tiles] = (
            body[:, 0:middle].reshape(quarter, tiles, 8, middle).astype(half)
        )
        x_out[pl.ds(first_to, quarter), tiles : 2 * tiles] = (
            body[:, middle:width].reshape(quarter, tiles, 8, middle).astype(half)
        )
        x_out[pl.ds(first_to, quarter), 2 * tiles] = tail.reshape(quarter, 8, middle).astype(half)

        def launch(j):
            to = first_to + lax.rem(me + j, quarter)

            @pl.when(to != me)
            def _():
                transfer(2, x_out, gin_got, to, me).start()

        steps_to(quarter, launch)

    steps_to(4, deliver)
    gin_got[me] = x_out[me]
    for w in range(turns, chunks // 2 + bits - 1):
        wave(w)

    def put(p):
        values = gin_got[p].astype(full)
        start = pl.multiple_of(p * spread, 8)
        for b in range(cuts):
            to, at = divmod(b, cuts // 2)
            at = slice(at * lanes, (at + 1) * lanes)
            flat[b, pl.ds(start, major), :] = values[to * tiles : (to + 1) * tiles, :, at].reshape(major, lanes)
            flat[b, pl.ds(start + major, minor), :] = values[2 * tiles, to * 4 : to * 4 + minor, at]

    def land(i):
        source = before(i + 1)
        arrived(2, x_out, gin_got, source)
        put(source)

    put(me)
    steps_to(n - 1, land)

    def write(c):
        for b in range(cuts):
            gin_ref[c, :, b * lanes : (b + 1) * lanes] = flat[b, pl.ds(c, n, stride=spread), :].astype(half)

    steps_to(per, write)

    def sums_sent(chunk, parity):
        for phase in range(bits):
            move(chunk, parity, phase).wait_send()

    for j in range(2):
        steps_to(chunks // 2, lambda i: sums_sent(2 * i + j, j))
    steps_to(n - 1, lambda i: transfer(2, x_out, gin_got, other(i + 1), me).wait_send())


def fused(n, block, cohorts, hidden_in, grad_out, norm_gain, w_qkv, w_out, sharpness, cohort_ids, observed):
    per, patches, width = hidden_in.shape
    heads = sharpness.shape[0]
    head_size = width // heads
    campaigns = per * n
    lanes = 128
    rows = block * cohorts
    cuts = width // lanes
    groups = cuts
    bits = n.bit_length() - 1
    major = per - per % 16
    slots = n * (major + 8)
    chunk_cols = 3 * lanes
    chunks = width // chunk_cols + groups
    piece = (width // n // 8, 8, chunk_cols)
    half, full = jnp.bfloat16, jnp.float32
    parcel = (n, major // 4 + 1, 8, width // 2)
    anywhere = pl.BlockSpec(memory_space=pl.ANY)
    vmem = pl.BlockSpec(memory_space=pltpu.VMEM)
    scratch = [
        pltpu.VMEM((per, patches, width), half),
        pltpu.VMEM((per, patches, width), half),
        pltpu.VMEM((width, 3 * width), half),
        pltpu.VMEM((width, width), half),
        pltpu.VMEM((cuts, max(per * patches, n * (per + 8 - per % 8)), lanes), full),
    ]
    scratch += [pltpu.VMEM(parcel, half)] * 5
    scratch += [
        pltpu.VMEM((n * 8, width // 2), full),
        pltpu.VMEM((slots, width), half),
        pltpu.VMEM((rows, slots), half),
        pltpu.VMEM((slots, rows), half),
        pltpu.VMEM((rows, lanes // head_size * block), full),
        pltpu.VMEM((rows, width), half),
        pltpu.VMEM((rows, width), half),
        pltpu.VMEM((width, rows), half),
        pltpu.VMEM((rows, width), half),
        pltpu.VMEM((rows, width), half),
        pltpu.VMEM((rows, width), half),
        pltpu.VMEM((rows, width), full),
        pltpu.VMEM((rows, width), full),
        pltpu.VMEM((groups * cohorts, block, lanes // head_size * block), half),
        pltpu.VMEM((cohorts, width, block), half),
        pltpu.VMEM((rows, width), half),
        pltpu.VMEM((rows, width), half),
        pltpu.VMEM((rows, 3 * width), half),
        pltpu.VMEM((chunks,) + (2,) * bits + piece, half),
    ]
    scratch += [pltpu.VMEM((chunks,) + (2,) * (bits - 1 - p) + piece, half) for p in range(bits)]
    scratch += [
        pltpu.SemaphoreType.DMA((4,)),
        pltpu.SemaphoreType.DMA((3, n)),
        pltpu.SemaphoreType.DMA((3, n)),
        pltpu.SemaphoreType.DMA((chunks, bits)),
        pltpu.SemaphoreType.DMA((chunks, bits)),
    ]
    return pl.pallas_call(
        functools.partial(fused_kernel, n, block, cohorts, head_size),
        in_specs=[pl.BlockSpec(memory_space=pltpu.SMEM)] + [anywhere] * 4 + [vmem] * 3,
        out_specs=[vmem] * 3,
        out_shape=[
            jax.ShapeDtypeStruct((per, n, width), half),
            jax.ShapeDtypeStruct((width // n, 3 * width), full),
            jax.ShapeDtypeStruct((width // n, width), full),
        ],
        scratch_shapes=scratch,
        compiler_params=pltpu.CompilerParams(
            collective_id=1, has_side_effects=True, vmem_limit_bytes=67_043_328
        ),
        cost_estimate=pl.CostEstimate(flops=60_000_000_000, bytes_accessed=12_000_000, transcendentals=0),
    )(
        sharpness,
        hidden_in,
        grad_out,
        w_qkv,
        w_out,
        norm_gain[None, :],
        cohort_ids[None, :],
        observed.T,
    )


def fits(n, hidden_in, sharpness, observed):
    per, patches, width = hidden_in.shape
    return (
        n >= 8
        and n & (n - 1) == 0
        and patches == n
        and per % 16 == 4
        and width % (n * 8) == 0
        and width % 768 == 0
        and sharpness.shape[0] * 64 == width
        and observed.shape[1] == 1
    )


def body(n, *args):
    hidden_in, sharpness, cohort_ids, observed = args[0], args[5], args[6], args[7]
    if not fits(n, hidden_in, sharpness, observed):
        return layer(n, *args)
    block = 64 * -(-6 * hidden_in.shape[0] * n // (5 * 64 * cohort_kinds))
    kinds = jnp.arange(cohort_kinds, dtype=cohort_ids.dtype)
    most = jnp.max(jnp.sum((cohort_ids[None, :] == kinds[:, None]).astype(jnp.int32), axis=1))
    crowded = lax.pmax((most > block).astype(jnp.int32), "grp") > 0
    return lax.cond(
        crowded,
        functools.partial(layer, n),
        functools.partial(fused, n, block, cohort_kinds),
        *args,
    )


def solution(mesh):
    in_specs = (
        P(("grp", "dev"), None, None),
        P(("grp", "dev"), None, None),
        P(),
        P(),
        P(),
        P(),
        P("grp"),
        P("grp", "dev"),
    )
    out_specs = (P(("grp", "dev"), None, None), P(("grp", "dev"), None), P(("grp", "dev"), None))
    step = jax.shard_map(functools.partial(body, mesh.shape["dev"]), mesh=mesh, in_specs=in_specs, out_specs=out_specs, check_vma=False)
    return step
```

```python
import functools
import math

import jax
import jax.numpy as jnp
from jax import lax
from jax.experimental import pallas as pl
from jax.experimental.pallas import tpu as pltpu
from jax.sharding import PartitionSpec as P

epsilon = 1e-06
log2e = math.log2(math.e)
cohort_kinds = 4


def dot(left, right, dims):
    return lax.dot_general(left, right, ((dims[0], dims[1]), ((), ())), preferred_element_type=jnp.float32)


def forward_kernel(
    head_size,
    group,
    sharp_ref,
    x_ref,
    gain_ref,
    wq_ref,
    wk_ref,
    wv_ref,
    cohort_col_ref,
    cohort_row_ref,
    seen_ref,
    normed_t_ref,
    q_ref,
    k_ref,
    k_t_ref,
    v_ref,
    inv_ref,
    probs_ref,
    att_ref,
    normed_ref,
    mask_ref,
):
    step = pl.program_id(0)
    rows, width = x_ref.shape

    @pl.when(step == 0)
    def _():
        values = x_ref[...].astype(jnp.float32)
        inv = lax.rsqrt(jnp.mean(values * values, axis=-1, keepdims=True) + epsilon)
        normed = values * inv * gain_ref[...]
        normed_ref[...] = normed.astype(jnp.bfloat16)
        normed_t_ref[...] = normed.T.astype(jnp.bfloat16)
        same = cohort_col_ref[...] == cohort_row_ref[...]
        diagonal = lax.broadcasted_iota(jnp.int32, (rows, rows), 0) == lax.broadcasted_iota(
            jnp.int32, (rows, rows), 1
        )
        seen = jnp.broadcast_to(seen_ref[...], (rows, rows)) == 1
        mask_ref[...] = jnp.where(same & (seen | diagonal), 1.0, 0.0)

    normed = normed_ref[...]
    q_raw = dot(normed, wq_ref[...], ((1,), (0,)))
    k_raw = dot(normed, wk_ref[...], ((1,), (0,)))
    v_raw = dot(normed, wv_ref[...], ((1,), (0,)))
    v_ref[...] = v_raw.astype(jnp.bfloat16)
    for h in range(group):
        base = h * head_size
        lanes = slice(base, base + head_size)
        q = q_raw[:, lanes]
        k = k_raw[:, lanes]
        v_t = v_raw[:, lanes].T.astype(jnp.bfloat16)
        q_inv = lax.rsqrt(jnp.mean(q * q, axis=-1, keepdims=True) + epsilon)
        k_inv = lax.rsqrt(jnp.mean(k * k, axis=-1, keepdims=True) + epsilon)
        q_half = (q * q_inv).astype(jnp.bfloat16)
        k_unit = k * k_inv
        k_half = k_unit.astype(jnp.bfloat16)
        k_t_ref[lanes, :] = k_unit.T.astype(jnp.bfloat16)
        q_ref[:, lanes] = q_half
        k_ref[:, lanes] = k_half
        inv_ref[0, :, h : h + 1] = q_inv
        inv_ref[0, :, group + h : group + h + 1] = k_inv
        scale = sharp_ref[step * group + h] / head_size
        scores = dot(k_half, q_half, ((1,), (1,)))
        weights = jnp.exp2(scores * (scale * log2e)) * mask_ref[...]
        probs = weights * (1.0 / jnp.sum(weights, axis=0, keepdims=True))
        probs_half = probs.astype(jnp.bfloat16)
        probs_ref[h] = probs_half
        att_ref[base : base + head_size, :] = dot(v_t, probs_half, ((1,), (0,))).astype(jnp.bfloat16)


def backward_kernel(
    head_size,
    group,
    sharp_ref,
    x_ref,
    dy_ref,
    gain_ref,
    wqkv_t_ref,
    wo_t_ref,
    q_ref,
    k_ref,
    k_t_ref,
    v_ref,
    inv_ref,
    probs_ref,
    gin_ref,
    dproj_ref,
):
    step = pl.program_id(0)
    gw = group * head_size
    width = x_ref.shape[1]
    da_half = dot(dy_ref[...], wo_t_ref[...], ((1,), (0,))).astype(jnp.bfloat16)
    parts = ([], [], [])
    for h in range(group):
        base = h * head_size
        lanes = slice(base, base + head_size)
        q_half = q_ref[:, lanes]
        q_unit = q_half.astype(jnp.float32)
        k_unit = k_ref[:, lanes].astype(jnp.float32)
        da = da_half[:, lanes]
        q_inv = inv_ref[0, :, h : h + 1]
        k_inv = inv_ref[0, :, group + h : group + h + 1]
        scale = sharp_ref[step * group + h] / head_size
        grad_probs = dot(v_ref[:, lanes], da, ((1,), (1,)))
        probs_half = probs_ref[h]
        probs = probs_half.astype(jnp.float32)
        grad_v = dot(probs_half, da, ((1,), (0,)))
        row_dot = jnp.sum(grad_probs * probs, axis=0, keepdims=True)
        grad_scores = (probs * (grad_probs - row_dot)).astype(jnp.bfloat16)
        dq = dot(k_t_ref[lanes, :], grad_scores, ((1,), (0,))).T * scale
        dk = dot(grad_scores, q_half, ((1,), (0,))) * scale
        dq = q_inv * (dq - q_unit * jnp.mean(dq * q_unit, axis=-1, keepdims=True))
        dk = k_inv * (dk - k_unit * jnp.mean(dk * k_unit, axis=-1, keepdims=True))
        for part, value in zip(parts, (dq, dk, grad_v)):
            part.append(value.astype(jnp.bfloat16))
    for at, part in enumerate(parts):
        start = pl.multiple_of(at * width + step * gw, gw)
        dproj_ref[:, pl.ds(start, gw)] = jnp.concatenate(part, axis=1)

    @pl.when(step == pl.num_programs(0) - 1)
    def _():
        values = x_ref[...].astype(jnp.float32)
        inv = lax.rsqrt(jnp.mean(values * values, axis=-1, keepdims=True) + epsilon)
        unit = values * inv
        shaped = dot(dproj_ref[...], wqkv_t_ref[...], ((1,), (0,))) * gain_ref[...]
        result = dy_ref[...].astype(jnp.float32) + inv * (
            shaped - unit * jnp.mean(shaped * unit, axis=-1, keepdims=True)
        )
        gin_ref[...] = result.astype(jnp.bfloat16)


def weights_kernel(normed_t_ref, att_ref, dq_ref, dk_ref, dv_ref, dy_ref, gqkv_ref, gwo_ref):
    dproj = jnp.concatenate([dq_ref[...], dk_ref[...], dv_ref[...]], axis=1)
    gqkv_ref[0] = dot(normed_t_ref[...], dproj, ((1,), (0,))).astype(jnp.bfloat16)
    gwo_ref[...] = dot(att_ref[...], dy_ref[...], ((1,), (0,))).astype(jnp.bfloat16)


def patch_grads(x, dy, norm_gain, w_qkv, w_out, sharpness, cohort_ids, seen):
    rows, width = x.shape
    heads = sharpness.shape[0]
    head_size = width // heads
    group = math.gcd(heads, 2)
    steps = heads // group
    gw = group * head_size
    half = jnp.bfloat16
    whole = lambda shape: pl.BlockSpec(shape, lambda g: (0,) * len(shape))
    cols = lambda n: pl.BlockSpec((rows, n), lambda g: (0, g))
    lines = lambda n: pl.BlockSpec((gw, n), lambda g: (g, 0))
    smem = pl.BlockSpec(memory_space=pltpu.SMEM)
    weights = [
        pl.BlockSpec((width, gw), lambda g: (0, g)),
        pl.BlockSpec((width, gw), lambda g: (0, steps + g)),
        pl.BlockSpec((width, gw), lambda g: (0, 2 * steps + g)),
    ]
    invs = pl.BlockSpec((1, rows, 2 * group), lambda g: (g, 0, 0))
    probs_spec = pl.BlockSpec((group, rows, rows), lambda g: (g, 0, 0))
    w_qkv_t, w_out_t = w_qkv.T, w_out.T
    params = pltpu.CompilerParams(vmem_limit_bytes=60 * 1024 * 1024)

    def cost(flops):
        return pl.CostEstimate(flops=flops, bytes_accessed=rows * width * 20, transcendentals=0)

    forward = pl.pallas_call(
        functools.partial(forward_kernel, head_size, group),
        grid=(steps,),
        in_specs=[smem, whole((rows, width)), whole((1, width))]
        + weights
        + [whole((rows, 1)), whole((1, rows)), whole((rows, 1))],
        out_specs=[whole((width, rows)), cols(gw), cols(gw), lines(rows), cols(gw), invs, probs_spec, lines(rows)],
        out_shape=[
            jax.ShapeDtypeStruct((width, rows), half),
            jax.ShapeDtypeStruct((rows, width), half),
            jax.ShapeDtypeStruct((rows, width), half),
            jax.ShapeDtypeStruct((width, rows), half),
            jax.ShapeDtypeStruct((rows, width), half),
            jax.ShapeDtypeStruct((steps, rows, 2 * group), jnp.float32),
            jax.ShapeDtypeStruct((heads, rows, rows), half),
            jax.ShapeDtypeStruct((width, rows), half),
        ],
        scratch_shapes=[
            pltpu.VMEM((rows, width), half),
            pltpu.VMEM((rows, rows), jnp.float32),
        ],
        compiler_params=params,
        cost_estimate=cost(40_000_000_000),
    )
    with jax.named_scope("forward_part"):
        normed_t, q, k, k_t, v, inv, probs, att = forward(
            sharpness,
            x,
            norm_gain[None, :],
            w_qkv,
            w_qkv,
            w_qkv,
            cohort_ids[:, None],
            cohort_ids[None, :],
            seen,
        )
    gin, dproj = pl.pallas_call(
        functools.partial(backward_kernel, head_size, group),
        grid=(steps,),
        in_specs=[
            smem,
            whole((rows, width)),
            whole((rows, width)),
            whole((1, width)),
            whole((3 * width, width)),
            pl.BlockSpec((width, gw), lambda g: (0, g)),
            cols(gw),
            cols(gw),
            lines(rows),
            cols(gw),
            invs,
            probs_spec,
        ],
        out_specs=[whole((rows, width)), whole((rows, 3 * width))],
        out_shape=[
            jax.ShapeDtypeStruct((rows, width), half),
            jax.ShapeDtypeStruct((rows, 3 * width), half),
        ],
        compiler_params=params,
        cost_estimate=cost(25_000_000_000),
    )(sharpness, x, dy, norm_gain[None, :], w_qkv_t, w_out_t, q, k, k_t, v, inv, probs)
    gqkv, gwo = pl.pallas_call(
        weights_kernel,
        grid=(steps,),
        in_specs=[
            whole((width, rows)),
            lines(rows),
            cols(gw),
            pl.BlockSpec((rows, gw), lambda g: (0, steps + g)),
            pl.BlockSpec((rows, gw), lambda g: (0, 2 * steps + g)),
            whole((rows, width)),
        ],
        out_specs=[pl.BlockSpec((1, width, 3 * gw), lambda g: (g, 0, 0)), lines(width)],
        out_shape=[
            jax.ShapeDtypeStruct((steps, width, 3 * gw), half),
            jax.ShapeDtypeStruct((width, width), half),
        ],
        compiler_params=pltpu.CompilerParams(vmem_limit_bytes=30 * 1024 * 1024),
        cost_estimate=cost(8_000_000_000),
    )(normed_t, att, dproj, dproj, dproj, dy)
    return gin, gqkv, gwo


def scatter_kernel(n, chunks, group_cols, qkv_ref, wo_ref, out_ref, wout_ref, *scratch):
    bits = n.bit_length() - 1
    recv = scratch[:bits]
    kept = (None,) + scratch[bits : 2 * bits - 1]
    send_sem, recv_sem = scratch[2 * bits - 1 :]
    me = lax.axis_index("dev")
    bit = [(me // (1 << b)) % 2 for b in range(bits)]
    peer = [me + (1 - 2 * bit[b]) * (1 << b) for b in range(bits)]
    groups = qkv_ref.shape[0]
    cols = qkv_ref.shape[-1]
    width = wout_ref.shape[-1]

    barrier = pltpu.get_barrier_semaphore()
    for b in range(bits):
        pl.semaphore_signal(
            barrier, inc=1, device_id={"dev": peer[b]}, device_id_type=pl.DeviceIdType.MESH
        )
    pl.semaphore_wait(barrier, bits)

    def order_of(chunk):
        order = list(range(bits))
        if chunk % 2 and bits > 2:
            order[1], order[2] = order[2], order[1]
        return order

    def source(chunk, phase, side):
        order = order_of(chunk)
        left = sorted(set(range(bits)) - set(order[:phase]), reverse=True)
        picks = tuple(side if b == order[phase] else slice(None) for b in left)
        if phase:
            return kept[phase], (chunk,) + picks
        if chunk < groups:
            return qkv_ref, (chunk,) + picks
        start = (chunk - groups) * cols
        return wo_ref, picks + (slice(None), slice(start, start + cols))

    copies = {}

    def begin(chunk, phase):
        b = order_of(chunk)[phase]
        ref, index = source(chunk, phase, 1 - bit[b])
        copy = pltpu.make_async_remote_copy(
            src_ref=ref.at[index],
            dst_ref=recv[phase].at[chunk],
            send_sem=send_sem.at[chunk, phase],
            recv_sem=recv_sem.at[chunk, phase],
            device_id={"dev": peer[b]},
            device_id_type=pl.DeviceIdType.MESH,
        )
        copy.start()
        copies[chunk, phase] = copy

    def finish(chunk, phase):
        b = order_of(chunk)[phase]
        copies[chunk, phase].wait_recv()
        ref, index = source(chunk, phase, bit[b])
        total = ref[index].astype(jnp.float32) + recv[phase][chunk].astype(jnp.float32)
        if phase + 1 < bits:
            kept[phase + 1][chunk] = total.astype(jnp.bfloat16)
            begin(chunk, phase + 1)
        elif chunk < groups:
            for part in range(3):
                at = part * width + chunk * group_cols
                out_ref[:, at : at + group_cols] = total[
                    :, part * group_cols : (part + 1) * group_cols
                ]
        else:
            at = (chunk - groups) * cols
            wout_ref[:, at : at + cols] = total

    for chunk in range(chunks):
        begin(chunk, 0)
    pairs = -(-chunks // 2)
    for wave in range(pairs + bits - 1):
        for phase in reversed(range(bits)):
            pair = wave - phase
            if 0 <= pair < pairs:
                for chunk in range(2 * pair, min(2 * pair + 2, chunks)):
                    finish(chunk, phase)
    for copy in copies.values():
        copy.wait_send()


def scatter_sums(gqkv, gwo, n):
    groups, width, cols = gqkv.shape
    bits = n.bit_length() - 1
    rows = width // n
    chunks = groups + width // cols
    cube = (2,) * bits
    recv = [pltpu.VMEM((chunks,) + (2,) * (bits - 1 - p) + (rows, cols), jnp.bfloat16) for p in range(bits)]
    kept = [pltpu.VMEM((chunks,) + (2,) * (bits - p) + (rows, cols), jnp.bfloat16) for p in range(1, bits)]
    vmem = pl.BlockSpec(memory_space=pltpu.VMEM)
    return pl.pallas_call(
        functools.partial(scatter_kernel, n, chunks, cols // 3),
        in_specs=[vmem, vmem],
        out_specs=[vmem, vmem],
        out_shape=[
            jax.ShapeDtypeStruct((rows, 3 * width), jnp.float32),
            jax.ShapeDtypeStruct((rows, width), jnp.float32),
        ],
        scratch_shapes=recv
        + kept
        + [pltpu.SemaphoreType.DMA((chunks, bits)), pltpu.SemaphoreType.DMA((chunks, bits))],
        compiler_params=pltpu.CompilerParams(
            collective_id=0, has_side_effects=True, vmem_limit_bytes=40 * 1024 * 1024
        ),
        cost_estimate=pl.CostEstimate(
            flops=40_000_000_000, bytes_accessed=8 * gqkv.size, transcendentals=0
        ),
    )(gqkv.reshape((groups,) + cube + (rows, cols)), gwo.reshape(cube + (rows, width)))


def layer(n, hidden_in, grad_out, norm_gain, w_qkv, w_out, sharpness, cohort_ids, observed):
    width = hidden_in.shape[-1]
    x = lax.all_to_all(hidden_in, "dev", split_axis=1, concat_axis=0, tiled=True)
    with jax.named_scope("cotangent_move"):
        dy = lax.all_to_all(grad_out, "dev", split_axis=1, concat_axis=0, tiled=True)
    campaigns, patches, _ = x.shape
    gin, gqkv, gwo = [], 0.0, 0.0
    for p in range(patches):
        a, b, c = patch_grads(
            x[:, p], dy[:, p], norm_gain, w_qkv, w_out, sharpness, cohort_ids, observed[:, p : p + 1]
        )
        gin.append(a.reshape(n, campaigns // n, width))
        gqkv, gwo = (b, c) if p == 0 else (gqkv + b, gwo + c)
    gin = gin[0] if patches == 1 else jnp.stack(gin, axis=1).reshape(n * patches, campaigns // n, width)
    grad_in = lax.all_to_all(gin, "dev", split_axis=0, concat_axis=0, tiled=True).transpose(1, 0, 2)
    grad_qkv, grad_wout = scatter_sums(gqkv, gwo, n)
    return (grad_in, grad_qkv, grad_wout)


def steps_to(total, body):
    lax.fori_loop(0, total, lambda i, c: (body(i), c)[1], 0)


def fused_kernel(
    n,
    block,
    cohorts,
    head_size,
    sharp_ref,
    x_hbm,
    dy_hbm,
    wqkv_hbm,
    wo_hbm,
    gain_ref,
    cohort_ref,
    seen_ref,
    gin_ref,
    gqkv_ref,
    gwo_ref,
    x_in,
    dy_in,
    wqkv_ref,
    wo_ref,
    flat,
    x_out,
    dy_out,
    x_got,
    dy_got,
    gin_got,
    tail_ref,
    got_ref,
    place_ref,
    place_t_ref,
    mask_ref,
    xs_ref,
    normed_ref,
    normed_t_ref,
    q_ref,
    k_ref,
    v_ref,
    q_inv_ref,
    k_inv_ref,
    probs_ref,
    att_ref,
    dys_ref,
    da_ref,
    dproj_ref,
    ones_ref,
    sums_ref,
    *rest,
):
    bits = n.bit_length() - 1
    recv = rest[:bits]
    local_sem, send_sem, recv_sem, sum_send, sum_recv = rest[bits:]
    half, full = jnp.bfloat16, jnp.float32
    per, patches, width = x_in.shape
    campaigns = per * n
    lanes = 128
    cuts = width // lanes
    middle = width // 2
    rows = block * cohorts
    heads = width // head_size
    quad = 2 * lanes
    pair = lanes // head_size
    groups = width // quad
    wide = 2 * pair * block
    major = per - per % 16
    minor = per % 16
    tiles = major // 8
    spread = per + 8 - per % 8
    me = lax.axis_index("dev")

    def other(i):
        return lax.rem(me + i, n)

    def before(i):
        return lax.rem(me + n - i, n)

    loads = [
        pltpu.make_async_copy(a, b, local_sem.at[i])
        for i, (a, b) in enumerate(((x_hbm, x_in), (dy_hbm, dy_in), (wqkv_hbm, wqkv_ref), (wo_hbm, wo_ref)))
    ]
    for load in loads:
        load.start()
    barrier = pltpu.get_barrier_semaphore()

    def greet(i):
        pl.semaphore_signal(
            barrier, inc=1, device_id={"dev": other(i + 1)}, device_id_type=pl.DeviceIdType.MESH
        )

    steps_to(n - 1, greet)

    def prepare(source, out):
        def widen(c):
            start = pl.multiple_of(c * patches, 8)
            for b in range(cuts):
                flat[b, pl.ds(start, patches), :] = source[c, :, b * lanes : (b + 1) * lanes].astype(full)

        def pick(p):
            for b in range(cuts):
                to, at = divmod(b, cuts // 2)
                at = slice(at * lanes, (at + 1) * lanes)
                body = flat[b, pl.ds(p, major, stride=patches), :].reshape(tiles, 8, lanes)
                out[p, to * tiles : (to + 1) * tiles, :, at] = body.astype(half)
            ends = []
            for b in range(cuts):
                ends.append(flat[b, pl.ds(major * patches + p, minor, stride=patches), :])
            for b in range(cuts // 2):
                both = jnp.concatenate([ends[b], ends[b + cuts // 2]], axis=0)
                out[p, 2 * tiles, :, b * lanes : (b + 1) * lanes] = both.astype(half)

        steps_to(per, widen)
        steps_to(n, pick)

    def transfer(kind, out, got, to, slot):
        return pltpu.make_async_remote_copy(
            src_ref=out.at[to],
            dst_ref=got.at[slot],
            send_sem=send_sem.at[kind, to],
            recv_sem=recv_sem.at[kind, slot],
            device_id={"dev": to},
            device_id_type=pl.DeviceIdType.MESH,
        )

    def send_all(kind, out, got):
        steps_to(n - 1, lambda i: transfer(kind, out, got, other(i + 1), me).start())

    def sent_all(kind, out, got):
        steps_to(n - 1, lambda i: transfer(kind, out, got, other(i + 1), me).wait_send())

    def arrived(kind, out, got, source):
        transfer(kind, out, got, source, source).wait_recv()

    loads[0].wait()
    prepare(x_in, x_out)
    pl.semaphore_wait(barrier, n - 1)
    send_all(0, x_out, x_got)
    x_got[me] = x_out[me]
    loads[1].wait()
    prepare(dy_in, dy_out)
    dy_got[me] = dy_out[me]
    send_all(1, dy_out, dy_got)

    cohort = cohort_ref[...].reshape(1, campaigns)
    line8 = jnp.broadcast_to(cohort.astype(full), (8, campaigns))
    column = line8.T[:, 0:1]
    same = (column == cohort.astype(full)) & (
        lax.broadcasted_iota(jnp.int32, (campaigns, campaigns), 0)
        < lax.broadcasted_iota(jnp.int32, (campaigns, campaigns), 1)
    )
    rank = jnp.sum(jnp.where(same, 1.0, 0.0), axis=0, keepdims=True)
    spot = cohort.astype(full) * block + rank
    high = jnp.floor(spot * (1 / 16))
    low = spot - 16 * high
    tags = jnp.concatenate(
        [high, low, seen_ref[...].astype(full), jnp.zeros((5, campaigns), full)], axis=0
    ).astype(half)
    slots = n * (major + 8)
    slot = lax.broadcasted_iota(jnp.int32, (1, slots), 1)
    after = slot - n * major
    in_major = slot < n * major
    first = in_major | (after % 8 < 4)
    owner = jnp.where(
        in_major, (slot // major) * per + slot % major, (after // 8) * per + major + after % minor
    )
    pick = jnp.where(lax.broadcasted_iota(jnp.int32, (campaigns, slots), 0) == owner, 1.0, 0.0)
    tags = dot(tags, pick.astype(half), ((1,), (0,)))
    spot = 16 * tags[0:1] + tags[1:2]
    spot8 = jnp.broadcast_to(spot, (8, slots))
    place = jnp.where(lax.broadcasted_iota(jnp.int32, (rows, slots), 0).astype(full) == spot, 1.0, 0.0)
    place_ref[...] = place.astype(half)
    place_t = jnp.where(lax.broadcasted_iota(jnp.int32, (slots, rows), 1).astype(full) == spot8.T[:, 0:1], 1.0, 0.0)
    place_t_ref[...] = place_t.astype(half)
    known = jnp.where(first, tags[2:3], 0.0)
    known = dot(place_ref[...], jnp.broadcast_to(known, (8, slots)).astype(half), ((1,), (1,)))[:, 0:1]
    for c in range(cohorts):
        row = lax.broadcasted_iota(jnp.int32, (block, block), 0)
        col = lax.broadcasted_iota(jnp.int32, (block, block), 1)
        mine = jnp.broadcast_to(known[c * block : (c + 1) * block], (block, block))
        square = jnp.where((row == col) | (mine > 0.5), 1.0, 0.0)
        mask_ref[c * block : (c + 1) * block, :] = jnp.concatenate([square] * pair, axis=1)

    lane = lax.broadcasted_iota(jnp.int32, (1, quad), 1) // head_size

    ones_row = lax.broadcasted_iota(jnp.int32, (quad, quad), 0) // head_size
    ones_col = lax.broadcasted_iota(jnp.int32, (quad, quad), 1) // head_size
    ones_ref[...] = jnp.where(ones_row == ones_col, 1.0 / head_size, 0.0).astype(half)

    def head_mean(values):
        return dot(values.astype(half), ones_ref[...], ((1,), (0,)))

    def split(values):
        return jnp.concatenate(
            [jnp.where(lane == h, values, jnp.zeros_like(values)) for h in range(2 * pair)], axis=0
        )

    def gather(kind, out, got):
        def take(source):
            values = got[source].astype(full)
            start = pl.multiple_of(source * major, 16)
            got_ref[pl.ds(start, major), 0:middle] = values[0:tiles].reshape(major, middle).astype(half)
            got_ref[pl.ds(start, major), middle:width] = (
                values[tiles : 2 * tiles].reshape(major, middle).astype(half)
            )
            tail_ref[pl.ds(pl.multiple_of(source * 8, 8), 8), :] = values[2 * tiles]

        def step(i):
            source = before(i + 1)
            arrived(kind, out, got, source)
            take(source)

        take(me)
        steps_to(n - 1, step)
        ends = tail_ref[...]
        upper = lax.broadcasted_iota(jnp.int32, ends.shape, 0) % 8 < 4
        start = n * major
        got_ref[start:, 0:middle] = jnp.where(upper, ends, 0.0).astype(half)
        got_ref[start:, middle:width] = jnp.where(upper, 0.0, ends).astype(half)

    loads[2].wait()
    loads[3].wait()
    gather(0, x_out, x_got)

    def settle(c):
        at = pl.ds(pl.multiple_of(c * block, block), block)
        values = dot(place_ref[at, :], got_ref[...], ((1,), (0,)))
        xs_ref[at, :] = values.astype(half)
        inv = lax.rsqrt(jnp.mean(values * values, axis=-1, keepdims=True) + epsilon)
        normed_ref[at, :] = (values * inv * gain_ref[...].reshape(1, width)).astype(half)

    steps_to(cohorts, settle)

    def turn(b):
        at = pl.ds(pl.multiple_of(b * lanes, lanes), lanes)
        normed_t_ref[at, :] = normed_ref[:, at].astype(full).T.astype(half)

    def quad_at(g, part=0):
        return pl.ds(pl.multiple_of(part * width + g * quad, quad), quad)

    def project(g):
        at = quad_at(g)
        for part, (unit_ref, inv_ref) in enumerate(((q_ref, q_inv_ref), (k_ref, k_inv_ref))):
            values = dot(normed_ref[...], wqkv_ref[:, quad_at(g, part)], ((1,), (0,)))
            inv = lax.rsqrt(head_mean(values * values) + epsilon)
            unit_ref[:, at] = (values * inv).astype(half)
            inv_ref[:, at] = inv
        v_ref[:, at] = dot(normed_ref[...], wqkv_ref[:, quad_at(g, 2)], ((1,), (0,))).astype(half)

    steps_to(groups, project)
    steps_to(cuts, turn)

    def scale_of(g, each):
        index = lax.broadcasted_iota(jnp.int32, (1, 2 * pair * each), 1) // each
        scale = jnp.zeros(index.shape, full)
        for h in range(2 * pair):
            scale = jnp.where(index == h, sharp_ref[g * 2 * pair + h] / head_size, scale)
        return scale

    def crossed(left, right):
        rows_of = []
        for i in range(2):
            values = dot(
                left[i * lanes : (i + 1) * lanes],
                right[:, i * pair * block : (i + 1) * pair * block],
                ((1,), (0,)),
            )
            for h in range(pair):
                rows_of.append(values[h * head_size : (h + 1) * head_size, h * block : (h + 1) * block])
        return jnp.concatenate(rows_of, axis=0)

    def attend(g):
        at = quad_at(g)
        scale = scale_of(g, block) * log2e
        for c in range(cohorts):
            block_rows = slice(c * block, (c + 1) * block)
            scores = dot(k_ref[block_rows, at], split(q_ref[block_rows, at]), ((1,), (1,)))
            mask = mask_ref[block_rows, :]
            weights = jnp.exp2(scores * scale) * jnp.concatenate([mask, mask], axis=1)
            probs = (weights * (1.0 / jnp.sum(weights, axis=0, keepdims=True))).astype(half)
            probs_ref[g * cohorts + c] = probs
            att_ref[c, at, :] = crossed(v_ref[block_rows, at].T, probs).astype(half)

    steps_to(groups, attend)

    gather(1, dy_out, dy_got)

    def settle_dy(c):
        at = pl.ds(pl.multiple_of(c * block, block), block)
        dys_ref[at, :] = dot(place_ref[at, :], got_ref[...], ((1,), (0,))).astype(half)

    steps_to(cohorts, settle_dy)

    bit = [(me // (1 << b)) % 2 for b in range(bits)]
    peer = [me + (1 - 2 * bit[b]) * (1 << b) for b in range(bits)]
    piece = sums_ref.shape[1 + bits :]
    chunk_cols = piece[-1]

    def order_of(parity):
        order = list(range(bits))
        if parity and bits > 2:
            order[1], order[2] = order[2], order[1]
        return order

    def view(chunk, parity, phase, side):
        order = order_of(parity)
        index = []
        for b in reversed(range(bits)):
            if b in order[:phase]:
                index.append(bit[b])
            elif b == order[phase]:
                index.append(side)
            else:
                index.append(slice(None))
        return (chunk,) + tuple(index)

    def move(chunk, parity, phase):
        b = order_of(parity)[phase]
        return pltpu.make_async_remote_copy(
            src_ref=sums_ref.at[view(chunk, parity, phase, 1 - bit[b])],
            dst_ref=recv[phase].at[chunk],
            send_sem=sum_send.at[chunk, phase],
            recv_sem=sum_recv.at[chunk, phase],
            device_id={"dev": peer[b]},
            device_id_type=pl.DeviceIdType.MESH,
        )

    def finish(chunk, parity, phase):
        b = order_of(parity)[phase]
        move(chunk, parity, phase).wait_recv()
        index = view(chunk, parity, phase, bit[b])
        total = sums_ref[index].astype(full) + recv[phase][chunk].astype(full)
        if phase + 1 < bits:
            sums_ref[index] = total.astype(half)
            move(chunk, parity, phase + 1).start()
        else:
            return total.reshape(width // n, chunk_cols)

    def keep(first_chunk, values):
        for j in range(2):
            part = values[:, j * chunk_cols : (j + 1) * chunk_cols]
            sums_ref[first_chunk + j] = part.reshape((2,) * bits + piece).astype(half)
        for j in range(2):
            move(first_chunk + j, j, 0).start()

    def finish_pair(at, phase):
        for j in range(2):
            finish(2 * at + j, j, phase)

    total = 0.0
    for c in range(cohorts):
        total += dot(att_ref[c], dys_ref[c * block : (c + 1) * block, :], ((1,), (0,)))
    keep(0, total)

    def spread_grad(b):
        at = pl.ds(pl.multiple_of(b * 2 * lanes, 2 * lanes), 2 * lanes)
        da_ref[:, at] = dot(dys_ref[...], wo_ref[at, :], ((1,), (1,))).astype(half)

    steps_to(cuts // 2, spread_grad)

    def settle_sums(at, phase):
        for j in range(2):
            chunk = 2 * at + j
            total = finish(chunk, j, phase)
            if phase + 1 < bits:
                continue
            for i in range(chunk_cols // lanes):
                values = total[:, i * lanes : (i + 1) * lanes]
                spot = j * (chunk_cols // lanes) + i
                if at == 0:
                    gwo_ref[:, spot * lanes : (spot + 1) * lanes] = values
                else:
                    start = spot // 2 * width + (at - 1) * quad + spot % 2 * lanes
                    gqkv_ref[:, start : start + lanes] = values

    def back(g):
        at = quad_at(g)
        scale = scale_of(g, head_size)
        for c in range(cohorts):
            block_rows = slice(c * block, (c + 1) * block)
            q, k, v = q_ref[block_rows, at], k_ref[block_rows, at], v_ref[block_rows, at]
            q_split = split(q)
            da_split = split(da_ref[block_rows, at])
            grad_probs = dot(v, da_split, ((1,), (1,)))
            probs_half = probs_ref[g * cohorts + c]
            probs = probs_half.astype(full)
            grad_v = dot(probs_half, da_split, ((1,), (0,)))
            row_dot = jnp.sum(grad_probs * probs, axis=0, keepdims=True)
            grad_scores = (probs * (grad_probs - row_dot)).astype(half)
            dk = dot(grad_scores, q_split, ((1,), (0,))) * scale
            dq = crossed(k.T, grad_scores).T * scale
            for part, (value, unit, inv_ref) in enumerate(((dq, q, q_inv_ref), (dk, k, k_inv_ref))):
                unit = unit.astype(full)
                value = inv_ref[block_rows, at] * (value - unit * head_mean(value * unit))
                dproj_ref[block_rows, quad_at(g, part)] = value.astype(half)
            dproj_ref[block_rows, quad_at(g, 2)] = grad_v.astype(half)
            for phase, lag, when in progress:
                if when == c and lag < groups:

                    @pl.when(g >= lag)
                    def _():
                        finish_pair(g - lag, phase)

        parts = [dproj_ref[:, quad_at(g, part)] for part in range(3)]
        keep(2 * g + 2, dot(normed_t_ref[...], jnp.concatenate(parts, axis=1), ((1,), (0,))))

    last = cohorts - 1
    progress = [(phase, phase, last) for phase in reversed(range(bits))]
    steps_to(groups, back)
    pairs = groups + 1

    def advance(turn, c):
        for phase, lag, when in progress:
            if when == c and 0 <= turn - lag < pairs:
                settle_sums(turn - lag, phase)

    def close(c):
        at = pl.ds(pl.multiple_of(c * block, block), block)
        values = xs_ref[at, :].astype(full)
        inv = lax.rsqrt(jnp.mean(values * values, axis=-1, keepdims=True) + epsilon)
        unit = values * inv
        shaped = dot(dproj_ref[at, :], wqkv_ref[...], ((1,), (1,))) * gain_ref[...].reshape(1, width)
        result = dys_ref[at, :].astype(full) + inv * (
            shaped - unit * jnp.mean(shaped * unit, axis=-1, keepdims=True)
        )
        xs_ref[at, :] = result.astype(half)

    for c in range(cohorts):
        close(c)
    sent_all(0, x_out, x_got)
    sent_all(1, dy_out, dy_got)
    quarter = n // 4

    def deliver(i):
        first_to = lax.rem(me // quarter + i, 4) * quarter
        at = pl.ds(pl.multiple_of(first_to * major, quarter * major), quarter * major)
        ends = pl.ds(pl.multiple_of(n * major + first_to * 8, quarter * 8), quarter * 8)
        body = dot(place_t_ref[at, :], xs_ref[...], ((1,), (0,)))
        tail = dot(place_t_ref[ends, :], xs_ref[...], ((1,), (0,)))
        upper = lax.broadcasted_iota(jnp.int32, (quarter * 8, middle), 0) % 8 < 4
        tail = jnp.where(upper, tail[:, 0:middle], tail[:, middle:width])
        x_out[pl.ds(first_to, quarter), 0:tiles] = (
            body[:, 0:middle].reshape(quarter, tiles, 8, middle).astype(half)
        )
        x_out[pl.ds(first_to, quarter), tiles : 2 * tiles] = (
            body[:, middle:width].reshape(quarter, tiles, 8, middle).astype(half)
        )
        x_out[pl.ds(first_to, quarter), 2 * tiles] = tail.reshape(quarter, 8, middle).astype(half)

        def launch(j):
            to = first_to + lax.rem(me + j, quarter)

            @pl.when(to != me)
            def _():
                transfer(2, x_out, gin_got, to, me).start()

        steps_to(quarter, launch)

    steps_to(4, deliver)
    gin_got[me] = x_out[me]
    for turn in range(groups, pairs + bits):
        for c in range(cohorts):
            advance(turn, c)

    def put(p):
        values = gin_got[p].astype(full)
        start = pl.multiple_of(p * spread, 8)
        for b in range(cuts):
            to, at = divmod(b, cuts // 2)
            at = slice(at * lanes, (at + 1) * lanes)
            flat[b, pl.ds(start, major), :] = values[to * tiles : (to + 1) * tiles, :, at].reshape(major, lanes)
            flat[b, pl.ds(start + major, minor), :] = values[2 * tiles, to * 4 : to * 4 + minor, at]

    def land(i):
        source = before(i + 1)
        arrived(2, x_out, gin_got, source)
        put(source)

    put(me)
    steps_to(n - 1, land)

    def write(c):
        for b in range(cuts):
            gin_ref[c, :, b * lanes : (b + 1) * lanes] = flat[b, pl.ds(c, n, stride=spread), :].astype(half)

    steps_to(per, write)

    def sums_sent(chunk, parity):
        for phase in range(bits):
            move(chunk, parity, phase).wait_send()

    for j in range(2):
        steps_to(pairs, lambda i: sums_sent(2 * i + j, j))
    steps_to(n - 1, lambda i: transfer(2, x_out, gin_got, other(i + 1), me).wait_send())


def fused(n, block, cohorts, hidden_in, grad_out, norm_gain, w_qkv, w_out, sharpness, cohort_ids, observed):
    per, patches, width = hidden_in.shape
    heads = sharpness.shape[0]
    head_size = width // heads
    campaigns = per * n
    lanes = 128
    rows = block * cohorts
    cuts = width // lanes
    groups = cuts // 2
    bits = n.bit_length() - 1
    major = per - per % 16
    slots = n * (major + 8)
    chunk_cols = 3 * lanes
    chunks = 2 + 2 * groups
    piece = (width // n // 8, 8, chunk_cols)
    half, full = jnp.bfloat16, jnp.float32
    parcel = (n, major // 4 + 1, 8, width // 2)
    anywhere = pl.BlockSpec(memory_space=pl.ANY)
    vmem = pl.BlockSpec(memory_space=pltpu.VMEM)
    scratch = [
        pltpu.VMEM((per, patches, width), half),
        pltpu.VMEM((per, patches, width), half),
        pltpu.VMEM((width, 3 * width), half),
        pltpu.VMEM((width, width), half),
        pltpu.VMEM((cuts, max(per * patches, n * (per + 8 - per % 8)), lanes), full),
    ]
    scratch += [pltpu.VMEM(parcel, half)] * 5
    scratch += [
        pltpu.VMEM((n * 8, width // 2), full),
        pltpu.VMEM((slots, width), half),
        pltpu.VMEM((rows, slots), half),
        pltpu.VMEM((slots, rows), half),
        pltpu.VMEM((rows, lanes // head_size * block), full),
        pltpu.VMEM((rows, width), half),
        pltpu.VMEM((rows, width), half),
        pltpu.VMEM((width, rows), half),
        pltpu.VMEM((rows, width), half),
        pltpu.VMEM((rows, width), half),
        pltpu.VMEM((rows, width), half),
        pltpu.VMEM((rows, width), full),
        pltpu.VMEM((rows, width), full),
        pltpu.VMEM((groups * cohorts, block, 2 * lanes // head_size * block), half),
        pltpu.VMEM((cohorts, width, block), half),
        pltpu.VMEM((rows, width), half),
        pltpu.VMEM((rows, width), half),
        pltpu.VMEM((rows, 3 * width), half),
        pltpu.VMEM((2 * lanes, 2 * lanes), half),
        pltpu.VMEM((chunks,) + (2,) * bits + piece, half),
    ]
    scratch += [pltpu.VMEM((chunks,) + (2,) * (bits - 1 - p) + piece, half) for p in range(bits)]
    scratch += [
        pltpu.SemaphoreType.DMA((4,)),
        pltpu.SemaphoreType.DMA((3, n)),
        pltpu.SemaphoreType.DMA((3, n)),
        pltpu.SemaphoreType.DMA((chunks, bits)),
        pltpu.SemaphoreType.DMA((chunks, bits)),
    ]
    return pl.pallas_call(
        functools.partial(fused_kernel, n, block, cohorts, head_size),
        in_specs=[pl.BlockSpec(memory_space=pltpu.SMEM)] + [anywhere] * 4 + [vmem] * 3,
        out_specs=[vmem] * 3,
        out_shape=[
            jax.ShapeDtypeStruct((per, n, width), half),
            jax.ShapeDtypeStruct((width // n, 3 * width), full),
            jax.ShapeDtypeStruct((width // n, width), full),
        ],
        scratch_shapes=scratch,
        compiler_params=pltpu.CompilerParams(
            collective_id=1, has_side_effects=True, vmem_limit_bytes=67_043_328
        ),
        cost_estimate=pl.CostEstimate(flops=60_000_000_000, bytes_accessed=12_000_000, transcendentals=0),
    )(
        sharpness,
        hidden_in,
        grad_out,
        w_qkv,
        w_out,
        norm_gain,
        cohort_ids,
        observed.T,
    )


def fits(n, hidden_in, sharpness, observed):
    per, patches, width = hidden_in.shape
    return (
        n >= 8
        and n & (n - 1) == 0
        and patches == n
        and per % 16 == 4
        and width % (n * 8) == 0
        and width % 768 == 0
        and sharpness.shape[0] * 64 == width
        and observed.shape[1] == 1
        and width // 256 < n.bit_length() - 1
    )


def body(n, *args):
    hidden_in, sharpness, cohort_ids, observed = args[0], args[5], args[6], args[7]
    if not fits(n, hidden_in, sharpness, observed):
        return layer(n, *args)
    block = 64 * -(-6 * hidden_in.shape[0] * n // (5 * 64 * cohort_kinds))
    kinds = jnp.arange(cohort_kinds, dtype=cohort_ids.dtype)
    most = jnp.max(jnp.sum((cohort_ids[None, :] == kinds[:, None]).astype(jnp.int32), axis=1))
    crowded = lax.pmax((most > block).astype(jnp.int32), "grp") > 0
    return lax.cond(
        crowded,
        functools.partial(layer, n),
        functools.partial(fused, n, block, cohort_kinds),
        *args,
    )


def solution(mesh):
    in_specs = (
        P(("grp", "dev"), None, None),
        P(("grp", "dev"), None, None),
        P(),
        P(),
        P(),
        P(),
        P("grp"),
        P("grp", "dev"),
    )
    out_specs = (P(("grp", "dev"), None, None), P(("grp", "dev"), None), P(("grp", "dev"), None))
    step = jax.shard_map(functools.partial(body, mesh.shape["dev"]), mesh=mesh, in_specs=in_specs, out_specs=out_specs, check_vma=False)
    return step
```
